32 devices in a mesh: row: 4 (over z), col: 8 (over y, x, core).
Axes of the slice: x: 2, y: 2, z: 4, core: 2. Of those that a mesh axis runs over, the one named last changes fastest.
Arguments:
- features: bfloat16 [8192, 512], P(('row', 'col')), may hold values from -6 to 6
- tile_values: bfloat16 [32, 16, 128, 128], P(('row', 'col')), may hold values from -0.21875 to 0.21875
- tile_blocks: int32 [32, 16, 2], P(('row', 'col')), may hold values from 0 to 63, as said below
- tile_count: int32 [32], P(('row', 'col')), may hold values from 1 to 16, as said below
- needed: int32 [32, 4], P(('row', 'col')), may hold values from 0 to 1
- weight_one: bfloat16 [512, 512], replicated, may hold values from -0.25 to 0.25
- weight_two: bfloat16 [512, 512], replicated, may hold values from -0.25 to 0.25
Outputs:
- nodes_out: bfloat16 [8192, 512], P(('row', 'col'))
The draws below stay inside these ranges and needn't reach their ends.
Inputs may be any that keep to these rules, and one draw needn't show every extreme that they name: `tile_blocks`: every row block of device d lies among the row blocks owned by the devices that share its index along row; for each device e along col in device d's row, all live or dead tiles of device d whose row block is owned by e name the same one of e's 2 blocks; the last device's first slot names the last block. `tile_count`: some device in every draw has all 16 slots live.
All inputs are finite; a program needn't handle non-finite values.
Results may differ from the reference program's by a relative error of at most 0.017.
Values may be sent and summed in bfloat16 or wider, within the bound.
No kernel may reach another device: no remote copies, remote signals or barrier semaphores. Data moves between devices by JAX's collectives and lax.ppermute only.
A program may use at most 64 MiB of HBM per device.

```python
import jax
import jax.numpy as jnp
from jax import lax

FEAT = 512
TILE = 128
BLK_DEV = 2
TMAX = 16
BLOCKS = 64
NODES = 8192
N_ROW = 4
N_COL = 8
DEVICES = 32


def draw_tile_blocks(key, part):
    first_key, second_key, third_key = jax.random.split(key, 3)
    device_ids = jnp.arange(DEVICES).astype(jnp.int32)
    row_of = device_ids // N_COL
    picks = jax.random.randint(first_key, (DEVICES, N_COL), 0, BLK_DEV).astype(jnp.int32)
    picks = picks.at[DEVICES - 1, N_COL - 1].set(BLK_DEV - 1)
    target = jax.random.randint(second_key, (DEVICES, TMAX), 0, N_COL).astype(jnp.int32)
    target = target.at[DEVICES - 1, 0].set(N_COL - 1)
    chosen = jnp.take_along_axis(picks, target, axis=1)
    row_blocks = (row_of[:, None] * N_COL + target) * BLK_DEV + chosen
    owners = jax.random.randint(third_key, (DEVICES, TMAX), 0, N_ROW).astype(jnp.int32)
    owners = owners.at[0, 0].set(0)
    return jnp.stack([row_blocks, owners], axis=-1).astype(jnp.int32)


def draw_tile_count(key, part):
    first_key, second_key, third_key = jax.random.split(key, 3)
    base_counts = jax.random.randint(first_key, (DEVICES,), max(1, TMAX // 8), TMAX // 2 + 1).astype(jnp.int32)
    heavy = jax.random.randint(second_key, (DEVICES,), 0, 8) == 0
    counts = jnp.where(heavy, TMAX, base_counts)
    spot = jax.random.randint(third_key, (), 0, DEVICES)
    counts = jnp.where(jnp.arange(DEVICES) == spot, TMAX, counts)
    return counts.astype(jnp.int32)


def touch_ends(result, rng, least, high):
    longest = result.shape.index(max(result.shape))
    spots = []
    for shift in (0, 1):
        where = [jax.random.randint(jax.random.fold_in(rng, axis), (), 0, length) for axis, length in enumerate(result.shape)]
        where[longest] = (where[longest] + shift) % result.shape[longest]
        spots.append(tuple(where))
    return result.at[spots[0]].set(least).at[spots[1]].set(high)


def block_scale(stream_key, dims, cuts, smallest, largest):
    def one(axis_at, parts):
        steps = jax.random.uniform(jax.random.fold_in(jax.random.fold_in(stream_key, 6), axis_at), (parts,), jnp.float32, smallest / len(cuts), largest / len(cuts))
        return jnp.repeat(jnp.exp(steps), dims[axis_at] // parts).reshape((-1,) + (1,) * (len(dims) - axis_at - 1))

    loudness = one(*cuts[0])
    for cut in cuts[1:]:
        loudness = loudness * one(*cut)
    return loudness


def normal_values(stream_key, extent, scale, most, pieces=(), kind=jnp.bfloat16):
    gain = block_scale(stream_key, extent, pieces, -0.22, 0.18) if pieces else 1.0
    values = jax.random.normal(stream_key, extent, jnp.float32) * scale * gain
    return jnp.minimum(jnp.maximum(values, -most), most).astype(kind)


def setup_inputs(seed: int = 0) -> dict:
    splits = jax.random.split(jax.random.key(seed), 8)
    return {
        "features": normal_values(splits[0], (NODES, FEAT), 1.0, 6.0, ((0, 32),)),
        "tile_values": normal_values(splits[1], (DEVICES, TMAX, TILE, TILE), (TILE * 6) ** -0.5, 0.21875, ((0, 32),)),
        "tile_blocks": draw_tile_blocks(jax.random.fold_in(splits[7], 71), 0),
        "tile_count": draw_tile_count(jax.random.fold_in(splits[7], 71), 0),
        "needed": touch_ends(jax.random.randint(splits[4], (DEVICES, N_ROW), 0, BLK_DEV), jax.random.fold_in(splits[4], 1), 0, BLK_DEV - 1).astype(jnp.int32),
        "weight_one": normal_values(splits[5], (FEAT, FEAT), FEAT ** -0.5, 0.25),
        "weight_two": normal_values(splits[6], (FEAT, FEAT), FEAT ** -0.5, 0.25),
    }


def aggregate(hidden, tile_values, tile_blocks, tile_count, needed):
    blocked = hidden.reshape(BLOCKS, TILE, FEAT)
    group_size = N_COL * BLK_DEV
    slot_ids = jnp.arange(TMAX).astype(jnp.int32)

    def device_step(device, totals):
        device = jnp.asarray(device).astype(jnp.int32)
        row_pos = device // N_COL
        col_pos = device % N_COL
        blocks_here = tile_blocks[device]
        source_owner = blocks_here[:, 1]
        column_block = (source_owner * N_COL + col_pos) * BLK_DEV + needed[device][source_owner]
        operands = blocked[column_block].astype(jnp.float32)
        adjacency = tile_values[device].astype(jnp.float32)
        products = jnp.einsum("tmk,tkf->tmf", adjacency, operands)
        alive = (slot_ids < tile_count[device]).astype(jnp.float32)
        products = products * alive[:, None, None]
        start = (row_pos * group_size).astype(jnp.int32)
        slot_index = (blocks_here[:, 0] - start).astype(jnp.int32)
        partial_value = jax.ops.segment_sum(products, slot_index, num_segments=group_size)
        partial_value = partial_value.astype(jnp.bfloat16).astype(jnp.float32)
        zero = jnp.zeros((), jnp.int32)
        current = lax.dynamic_slice(totals, (start, zero, zero), (group_size, TILE, FEAT))
        return lax.dynamic_update_slice(totals, current + partial_value, (start, zero, zero))

    totals = lax.fori_loop(0, DEVICES, device_step, jnp.zeros((BLOCKS, TILE, FEAT), jnp.float32))
    return totals.astype(jnp.bfloat16).reshape(NODES, FEAT)


def reference(features, tile_values, tile_blocks, tile_count, needed, weight_one, weight_two):
    mixed = aggregate(features, tile_values, tile_blocks, tile_count, needed)
    hidden = jnp.maximum(jnp.dot(mixed, weight_one, preferred_element_type=jnp.float32), 0.0).astype(jnp.bfloat16)
    mixed_two = aggregate(hidden, tile_values, tile_blocks, tile_count, needed)
    return jnp.dot(mixed_two, weight_two, preferred_element_type=jnp.float32).astype(jnp.bfloat16)
```

```python
import jax
import jax.numpy as jnp
from jax import lax
from jax.experimental import pallas as pl
from jax.experimental.pallas import tpu as pltpu
from jax.sharding import PartitionSpec as P


def build_kernel(dest_ref, source_ref, own_ref, peer_ref, out_ref, acc_ref):
    chip = pl.program_id(0)
    per_device, sources, tile, _ = acc_ref.shape
    slots = own_ref.shape[0]
    acc_ref[...] = jnp.zeros_like(acc_ref)
    for base, tiles in ((0, own_ref), (slots, peer_ref)):

        def add(t, carry, base=base, tiles=tiles):
            dest = dest_ref[base + t]

            @pl.when(dest // per_device == chip)
            def _():
                b = dest % per_device
                s = source_ref[base + t]
                acc_ref[b, s] = acc_ref[b, s] + tiles[t].astype(jnp.float32)

            return carry

        lax.fori_loop(0, slots, add, 0)
    for b in range(per_device):
        for s in range(sources):
            out_ref[0, b * tile : (b + 1) * tile, s * tile : (s + 1) * tile] = acc_ref[b, s].astype(out_ref.dtype)


def build_dense(dest, source, own_tiles, peer_tiles, chips, per_device, sources):
    slots, tile, _ = own_tiles.shape
    whole = pl.BlockSpec((slots, tile, tile), lambda i, *_: (0, 0, 0))
    return pl.pallas_call(
        build_kernel,
        grid_spec=pltpu.PrefetchScalarGridSpec(
            num_scalar_prefetch=2,
            grid=(chips,),
            in_specs=[whole, whole],
            out_specs=pl.BlockSpec((1, per_device * tile, sources * tile), lambda i, *_: (i, 0, 0)),
            scratch_shapes=[pltpu.VMEM((per_device, sources, tile, tile), jnp.float32)],
        ),
        out_shape=jax.ShapeDtypeStruct((chips, per_device * tile, sources * tile), own_tiles.dtype),
        name="build_dense",
    )(dest, source, own_tiles, peer_tiles)


def body(features, tile_values, tile_blocks, tile_count, needed, weight_one, weight_two):
    row_count = lax.axis_size("row")
    col_count = lax.axis_size("col")
    row_pos = lax.axis_index("row")
    col_pos = lax.axis_index("col")
    chips = col_count // 2
    core = col_pos % 2
    chip_pos = col_pos // 2
    tiles = tile_values[0]
    blocks_here = tile_blocks[0]
    slots, tile, _ = tiles.shape
    per_device = features.shape[0] // tile
    sources = 2 * row_count
    swap = [(i, i ^ 1) for i in range(col_count)]

    owner = blocks_here[:, 0] // per_device % col_count
    alive = jnp.arange(slots, dtype=jnp.int32) < tile_count[0]
    dest = ((owner // 2) ^ chip_pos) * per_device + blocks_here[:, 0] % per_device
    source = (row_pos - blocks_here[:, 1]) % row_count
    dest_own = jnp.where(alive & (owner % 2 == core), dest, -1)
    dest_peer = jnp.where(alive & (owner % 2 != core), dest, -1)
    info = lax.ppermute(jnp.stack([dest_peer, source]), "col", swap)
    peer_tiles = lax.ppermute(tiles, "col", swap)
    dense = build_dense(
        jnp.concatenate([dest_own, info[0]]),
        jnp.concatenate([source, info[1] + row_count]),
        tiles,
        peer_tiles,
        chips,
        per_device,
        sources,
    )

    wanted = [needed[0, row_pos]]
    for shift in range(1, row_count):
        peer = (row_pos - shift) % row_count
        wanted.append(
            lax.ppermute(
                needed[0, peer][None, None], "row", [(i, (i - shift) % row_count) for i in range(row_count)]
            )[0, 0]
        )

    def aggregate(values):
        width = values.shape[1]
        panel = []
        for shift in range(row_count):
            piece = lax.dynamic_slice(values, (wanted[shift] * tile, 0), (tile, width))
            if shift:
                piece = lax.ppermute(piece, "row", [(i, (i + shift) % row_count) for i in range(row_count)])
            panel.append(piece)
        panel = jnp.concatenate(panel, axis=0)
        other = lax.ppermute(panel, "col", swap)
        operand = jnp.concatenate([panel, other], axis=0)
        total = None
        for rel in range(chips):
            part = jnp.dot(dense[rel], operand, preferred_element_type=jnp.float32)
            if rel:
                part = lax.ppermute(
                    part.astype(jnp.bfloat16), "col", [(i, i ^ (2 * rel)) for i in range(col_count)]
                ).astype(jnp.float32)
            total = part if total is None else total + part
        return total

    mixed = jnp.dot(features, weight_one, preferred_element_type=jnp.float32).astype(jnp.bfloat16)
    hidden = jnp.maximum(aggregate(mixed), 0.0).astype(jnp.bfloat16)
    mixed = aggregate(hidden).astype(jnp.bfloat16)
    return jnp.dot(mixed, weight_two, preferred_element_type=jnp.float32).astype(jnp.bfloat16)


def solution(mesh):
    placed = (
        P(("row", "col"), None),
        P(("row", "col"), None, None, None),
        P(("row", "col"), None, None),
        P(("row", "col")),
        P(("row", "col"), None),
        P(),
        P(),
    )
    return jax.shard_map(
        body, mesh=mesh, in_specs=placed, out_specs=P(("row", "col"), None), check_vma=False
    )
```

```python
import jax
import jax.numpy as jnp
from jax import lax
from jax.experimental import pallas as pl
from jax.experimental.pallas import tpu as pltpu
from jax.sharding import PartitionSpec as P

CHUNKS = 1
SMEM = pl.BlockSpec(memory_space=pltpu.SMEM)
VMEM = pl.BlockSpec(memory_space=pltpu.VMEM)
HALF = jnp.bfloat16
FULL = jnp.float32


def build_kernel(own_at, peer_at, own_count, peer_count, own_tiles, peer_tiles, dense, picks):
    _, owners, tile, _ = dense.shape
    per_device = 2
    rows = dense.shape[3] // tile
    row_pos = lax.axis_index("row")
    col_pos = lax.axis_index("col")
    dense[...] = jnp.zeros_like(dense)
    for r, at, count, tiles in ((0, own_at, own_count, own_tiles), (1, peer_at, peer_count, peer_tiles)):
        for e in range(owners):
            picks[r, e] = 0

        def add(t, carry, r=r, at=at, tiles=tiles):
            block = at[0, t, 0]
            e = ((block // per_device) % owners) ^ col_pos
            s = (at[0, t, 1] % rows) ^ row_pos
            picks[r, e] = block % per_device
            cols = pl.ds(pl.multiple_of(s * tile, tile), tile)
            dense[r, e, :, cols] = (dense[r, e, :, cols].astype(FULL) + tiles[0, t].astype(FULL)).astype(HALF)
            return carry

        lax.fori_loop(0, count[0], add, 0)


def project_kernel(own, peer, weight, *outs):
    half = weight.shape[1] // 2
    width = half // len(outs)
    core = lax.axis_index("col") % 2
    for j, out in enumerate(outs):
        columns = weight[:, pl.ds(pl.multiple_of(core * half + j * width, width), width)]
        for r, x in enumerate((own, peer)):
            product = jnp.dot(x[...], columns, preferred_element_type=FULL).astype(HALF)
            out[r] = product.reshape(out.shape[1:])


def select_kernel(*refs):
    rows = (len(refs) - 1) // 2
    wanted, values, outs = refs[:rows], refs[rows], refs[rows + 1 :]
    row_pos = lax.axis_index("row")
    for s, out in enumerate(outs):
        for r in range(2):
            out[r] = values[r, wanted[s][r, row_pos]]


def multiply_kernel(*refs):
    picks, dense = refs[:2]
    _, owners, tile, depth = dense.shape
    rows = depth // tile
    pieces, outs = refs[2 : 2 + rows], refs[2 + rows :]
    operands = [jnp.concatenate([piece[r] for piece in pieces], axis=0) for r in range(2)]
    for e in range(owners):
        own = jnp.dot(dense[0, e], operands[0], preferred_element_type=FULL)
        peer = jnp.dot(dense[1, e], operands[1], preferred_element_type=FULL)
        for b in range(2):
            total = jnp.where(picks[0, e] == b, own, 0.0) + jnp.where(picks[1, e] == b, peer, 0.0)
            outs[e // 2][e % 2, b] = total.astype(HALF)


def added(parts, r, b):
    total = parts[0][r, b].astype(FULL)
    for part in parts[1:]:
        total = total + part[r, b].astype(FULL)
    return total


def hidden_kernel(*refs):
    values = refs[-1]
    rows = CHIPS_ROWS[1]
    wanted, parts, outs = refs[:rows], refs[rows : rows + CHIPS_ROWS[0]], refs[rows + CHIPS_ROWS[0] : -1]
    for r in range(2):
        for b in range(2):
            values[r, b] = jnp.maximum(added(parts, r, b), 0.0).astype(HALF)
    select_kernel(*wanted, values, *outs)


def mixed_kernel(*refs):
    parts, own, peer = refs[:-2], refs[-2], refs[-1]
    for b in range(2):
        own[b] = added(parts, 0, b).astype(HALF)
        peer[b] = added(parts, 1, b).astype(HALF)


def final_kernel(*refs):
    weight, out = refs[-2:]
    chunks = (len(refs) - 2) // 2
    half = weight.shape[0] // 2
    width = half // chunks
    core = lax.axis_index("col") % 2
    total = None
    for side in range(2):
        for j in range(chunks):
            x = refs[side * chunks + j][...].reshape(out.shape[0], width)
            at = pl.multiple_of((core ^ side) * half + j * width, width)
            product = jnp.dot(x, weight[pl.ds(at, width), :], preferred_element_type=FULL)
            total = product if total is None else total + product
    out[...] = total.astype(HALF)


CHIPS_ROWS = [0, 0]


def body(features, tile_values, tile_blocks, tile_count, needed, weight_one, weight_two):
    row_count = lax.axis_size("row")
    col_count = lax.axis_size("col")
    chips = col_count // 2
    CHIPS_ROWS[:] = [chips, row_count]
    _, slots, tile, _ = tile_values.shape
    feat = features.shape[1]
    width = feat // 2 // CHUNKS
    limit = min(60, 12 + 3 * (col_count * row_count * tile * tile) // 2**19) * 2**20
    swap_pairs = [(i, i ^ 1) for i in range(col_count)]

    def swap(x):
        return lax.ppermute(x, "col", swap_pairs)

    def by_row(x, s):
        return lax.ppermute(x, "row", [(i, i ^ s) for i in range(row_count)])

    def by_chip(x, c):
        return lax.ppermute(x, "col", [(i, i ^ (2 * c)) for i in range(col_count)])

    def shape(*dims):
        return jax.ShapeDtypeStruct(dims, HALF)

    both_needed = jnp.concatenate([needed, swap(needed)], axis=0)
    wanted = [both_needed] + [by_row(both_needed, s) for s in range(1, row_count)]
    peer_features = swap(features)
    dense, picks = pl.pallas_call(
        build_kernel,
        in_specs=[SMEM] * 4 + [VMEM] * 2,
        out_specs=[VMEM, SMEM],
        out_shape=[shape(2, col_count, tile, row_count * tile), jax.ShapeDtypeStruct((2, col_count), jnp.int32)],
        cost_estimate=pl.CostEstimate(flops=1_000_000_000, bytes_accessed=4_000_000, transcendentals=0),
        compiler_params=pltpu.CompilerParams(vmem_limit_bytes=limit),
        name="build",
    )(tile_blocks, swap(tile_blocks), tile_count, swap(tile_count), tile_values, swap(tile_values))
    projected = pl.pallas_call(
        project_kernel,
        in_specs=[VMEM] * 3,
        out_specs=[VMEM] * CHUNKS,
        out_shape=[shape(2, 2, tile, width)] * CHUNKS,
        compiler_params=pltpu.CompilerParams(vmem_limit_bytes=limit),
        name="project",
    )(features, peer_features, weight_one)

    piece = shape(2, tile, width)
    part = shape(2, 2, tile, width)

    def to_readers(pieces):
        return [x if s == 0 else by_row(x, s) for s, x in enumerate(pieces)]

    def to_owners(pieces):
        parts = pl.pallas_call(
            multiply_kernel,
            in_specs=[SMEM] + [VMEM] * (1 + row_count),
            out_specs=[VMEM] * chips,
            out_shape=[part] * chips,
            compiler_params=pltpu.CompilerParams(vmem_limit_bytes=limit),
        name="multiply",
        )(picks, dense, *pieces)
        return [x if c == 0 else by_chip(x, c) for c, x in enumerate(parts)]

    pieces = []
    for values in projected:
        chosen = pl.pallas_call(
            select_kernel,
            in_specs=[SMEM] * row_count + [VMEM],
            out_specs=[VMEM] * row_count,
            out_shape=[piece] * row_count,
            compiler_params=pltpu.CompilerParams(vmem_limit_bytes=limit),
        name="select",
        )(*wanted, values)
        pieces.append(to_readers(chosen))
    arrived = [to_owners(x) for x in pieces]
    pieces = []
    for parts in arrived:
        chosen = pl.pallas_call(
            hidden_kernel,
            in_specs=[SMEM] * row_count + [VMEM] * chips,
            out_specs=[VMEM] * row_count,
            out_shape=[piece] * row_count,
            scratch_shapes=[pltpu.VMEM((2, 2, tile, width), HALF)],
            compiler_params=pltpu.CompilerParams(vmem_limit_bytes=limit),
        name="hidden",
        )(*wanted, *parts)
        pieces.append(to_readers(chosen))
    arrived = [to_owners(x) for x in pieces]
    own, other = [], []
    for parts in arrived:
        mine, theirs = pl.pallas_call(
            mixed_kernel,
            in_specs=[VMEM] * chips,
            out_specs=[VMEM] * 2,
            out_shape=[shape(2, tile, width)] * 2,
            compiler_params=pltpu.CompilerParams(vmem_limit_bytes=limit),
        name="mixed",
        )(*parts)
        own.append(mine)
        other.append(swap(theirs))
    return pl.pallas_call(
        final_kernel,
        in_specs=[VMEM] * (2 * CHUNKS + 1),
        out_specs=VMEM,
        out_shape=shape(*features.shape),
        compiler_params=pltpu.CompilerParams(vmem_limit_bytes=limit),
        name="final",
    )(*own, *other, weight_two)


def solution(mesh):
    placed = (
        P(("row", "col"), None),
        P(("row", "col"), None, None, None),
        P(("row", "col"), None, None),
        P(("row", "col")),
        P(("row", "col"), None),
        P(),
        P(),
    )
    return jax.shard_map(
        body, mesh=mesh, in_specs=placed, out_specs=P(("row", "col"), None), check_vma=False
    )
```

```python
import functools

import jax
import jax.numpy as jnp
from jax import lax
from jax.experimental import pallas as pl
from jax.experimental.pallas import tpu as pltpu
from jax.sharding import PartitionSpec as P

CHUNKS = 2
SMEM = pl.BlockSpec(memory_space=pltpu.SMEM)
VMEM = pl.BlockSpec(memory_space=pltpu.VMEM)
HALF = jnp.bfloat16
FULL = jnp.float32


def build_kernel(own_at, peer_at, own_count, peer_count, own_tiles, peer_tiles, dense, picks):
    _, owners, tile, _ = dense.shape
    per_device = 2
    rows = dense.shape[3] // tile
    row_pos = lax.axis_index("row")
    col_pos = lax.axis_index("col")
    dense[...] = jnp.zeros_like(dense)
    for r, at, count, tiles in ((0, own_at, own_count, own_tiles), (1, peer_at, peer_count, peer_tiles)):
        for e in range(owners):
            picks[r, e] = 0

        def add(t, carry, r=r, at=at, tiles=tiles):
            block = at[0, t, 0]
            e = ((block // per_device) % owners) ^ col_pos
            s = (at[0, t, 1] % rows) ^ row_pos
            picks[r, e] = block % per_device
            cols = pl.ds(pl.multiple_of(s * tile, tile), tile)
            dense[r, e, :, cols] = (dense[r, e, :, cols].astype(FULL) + tiles[0, t].astype(FULL)).astype(HALF)
            return carry

        lax.fori_loop(0, count[0], add, 0)


def project_kernel(own, peer, weight, out):
    width = weight.shape[1] // 2
    core = lax.axis_index("col") % 2
    columns = weight[:, pl.ds(pl.multiple_of(core * width, width), width)]
    for r, x in enumerate((own, peer)):
        product = jnp.dot(x[...], columns, preferred_element_type=FULL).astype(HALF)
        out[r] = product.reshape(out.shape[1:])


def select(wanted, values, outs):
    row_pos = lax.axis_index("row")
    for s, out in enumerate(outs):
        for r in range(2):
            out[r] = values[r, wanted[s][r, row_pos]]


def select_kernel(*refs):
    rows = (len(refs) - 1) // 2
    select(refs[:rows], refs[rows], refs[rows + 1 :])


def multiply_kernel(*refs):
    picks, dense = refs[:2]
    _, owners, tile, depth = dense.shape
    rows = depth // tile
    pieces, outs = refs[2 : 2 + rows], refs[2 + rows :]
    chips = owners // 2
    columns = outs[0].shape[-1]
    ordered = pieces[:1] + pieces[:0:-1]
    operands = [jnp.concatenate([piece[r] for piece in ordered], axis=0) for r in range(2)]
    for e in range(owners):
        own = jnp.dot(dense[0, e], operands[0], preferred_element_type=FULL)
        peer = jnp.dot(dense[1, e], operands[1], preferred_element_type=FULL)
        for b in range(2):
            total = jnp.where(picks[0, e] == b, own, 0.0) + jnp.where(picks[1, e] == b, peer, 0.0)
            for j in range(len(outs) // chips):
                outs[j * chips + e // 2][e % 2, b] = total[:, j * columns : (j + 1) * columns].astype(HALF)


def added(parts, r, b):
    total = parts[0][r, b].astype(FULL)
    for part in parts[1:]:
        total = total + part[r, b].astype(FULL)
    return total


def hidden_kernel(*refs, rows):
    values = refs[-1]
    wanted, parts, outs = refs[:rows], refs[rows : -1 - rows], refs[-1 - rows : -1]
    for r in range(2):
        for b in range(2):
            values[r, b] = jnp.maximum(added(parts, r, b), 0.0).astype(HALF)
    select(wanted, values, outs)


def mixed_kernel(*refs):
    parts, own, peer = refs[:-2], refs[-2], refs[-1]
    for b in range(2):
        own[b] = added(parts, 0, b).astype(HALF)
        peer[b] = added(parts, 1, b).astype(HALF)


def final_kernel(*refs):
    weight, out = refs[-2:]
    sides = refs[: len(refs) // 2 - 1], refs[len(refs) // 2 - 1 : -2]
    core = lax.axis_index("col") % 2
    total = None
    for side, chunks in enumerate(sides):
        at = (core ^ side) * (weight.shape[0] // 2)
        for x in chunks:
            width = x.shape[-1]
            rows = x[...].reshape(out.shape[0], width)
            columns = weight[pl.ds(pl.multiple_of(at, width), width), :]
            product = jnp.dot(rows, columns, preferred_element_type=FULL)
            total = product if total is None else total + product
            at = at + width
    out[...] = total.astype(HALF)


def body(features, tile_values, tile_blocks, tile_count, needed, weight_one, weight_two):
    row_count = lax.axis_size("row")
    col_count = lax.axis_size("col")
    chips = col_count // 2
    _, slots, tile, _ = tile_values.shape
    width = features.shape[1] // 2
    limit = min(60, 12 + 3 * (col_count * row_count * tile * tile) // 2**19) * 2**20

    def call(kernel, out_shape, args, in_specs=None, out_specs=None, **options):
        many = isinstance(out_shape, list)
        return pl.pallas_call(
            kernel,
            in_specs=in_specs or [VMEM] * len(args),
            out_specs=out_specs or ([VMEM] * len(out_shape) if many else VMEM),
            out_shape=out_shape,
            compiler_params=pltpu.CompilerParams(vmem_limit_bytes=limit),
            cost_estimate=pl.CostEstimate(flops=1_000_000_000, bytes_accessed=10_000_000, transcendentals=0),
            **options,
        )(*args)

    def by_col(x, masks):
        return lax.ppermute(x, "col", [(i, i ^ masks[i % 2]) for i in range(col_count)])

    def swap(x):
        return by_col(x, (1, 1))

    def by_row(x, s):
        return lax.ppermute(x, "row", [(i, i ^ s) for i in range(row_count)])

    def shape(*dims, dtype=HALF):
        return jax.ShapeDtypeStruct(dims, dtype)

    both_needed = jnp.concatenate([needed, swap(needed)], axis=0)
    wanted = [both_needed] + [by_row(both_needed, s) for s in range(1, row_count)]
    projected = call(project_kernel, shape(2, 2, tile, width), [features, swap(features), weight_one], name="project")
    dense, picks = call(
        build_kernel,
        [shape(2, col_count, tile, row_count * tile), shape(2, col_count, dtype=jnp.int32)],
        [tile_blocks, swap(tile_blocks), tile_count, swap(tile_count), tile_values, swap(tile_values)],
        in_specs=[SMEM] * 4 + [VMEM] * 2,
        out_specs=[VMEM, SMEM],
        name="build",
    )

    columns = width // CHUNKS

    def to_readers(pieces):
        return [pieces[0]] + [by_row(pieces[s], s) for s in range(row_count - 1, 0, -1)]

    def to_owners(pieces):
        chunks = pieces[0].shape[-1] // columns
        parts = call(
            multiply_kernel,
            [shape(2, 2, tile, columns)] * (chips * chunks),
            [picks, dense, *pieces],
            in_specs=[SMEM] + [VMEM] * (1 + row_count),
            name="multiply",
        )
        parts = [parts[j * chips : (j + 1) * chips] for j in range(chunks)]
        return [[x[0]] + [by_col(x[c], (2 * c, 2 * c)) for c in range(1, chips)] for x in parts]

    selected = call(
        select_kernel,
        [shape(2, tile, width)] * row_count,
        [*wanted, projected],
        in_specs=[SMEM] * row_count + [VMEM],
        name="select",
    )
    arrived = to_owners(to_readers(selected))
    panels = []
    for parts in arrived:
        selected = call(
            functools.partial(hidden_kernel, rows=row_count),
            [shape(2, tile, columns)] * row_count,
            [*wanted, *parts],
            in_specs=[SMEM] * row_count + [VMEM] * len(parts),
            scratch_shapes=[pltpu.VMEM((2, 2, tile, columns), HALF)],
            name="hidden",
        )
        panels.append(to_readers(selected))
    arrived = [to_owners(panel)[0] for panel in panels]
    mine, theirs = [], []
    for parts in arrived:
        own, other = call(mixed_kernel, [shape(2, tile, columns)] * 2, parts, name="mixed")
        mine.append(own)
        theirs.append(swap(other))
    return call(final_kernel, shape(*features.shape), [*mine, *theirs, weight_two], name="final")


def solution(mesh):
    placed = (
        P(("row", "col"), None),
        P(("row", "col"), None, None, None),
        P(("row", "col"), None, None),
        P(("row", "col")),
        P(("row", "col"), None),
        P(),
        P(),
    )
    return jax.shard_map(
        body, mesh=mesh, in_specs=placed, out_specs=P(("row", "col"), None), check_vma=False
    )
```

```python
import functools

import jax
import jax.numpy as jnp
from jax import lax
from jax.experimental import pallas as pl
from jax.experimental.pallas import tpu as pltpu
from jax.sharding import PartitionSpec as P

CHUNKS = 2
FLOPS = 1_000_000_000
SMEM = pl.BlockSpec(memory_space=pltpu.SMEM)
VMEM = pl.BlockSpec(memory_space=pltpu.VMEM)
HALF = jnp.bfloat16
FULL = jnp.float32


def build_kernel(own_table, peer_table, own_tiles, peer_tiles, dense, picks):
    _, owners, tile, _ = dense.shape
    slots = own_tiles.shape[1]
    per_device = 2
    rows = dense.shape[3] // tile
    row_pos = lax.axis_index("row")
    col_pos = lax.axis_index("col")
    dense[...] = jnp.zeros_like(dense)
    picks[...] = jnp.zeros_like(picks)
    for r, table, tiles in ((0, own_table, own_tiles), (1, peer_table, peer_tiles)):

        def add(t, carry, r=r, table=table, tiles=tiles):
            block = table[2 * t]
            e = ((block // per_device) % owners) ^ col_pos
            s = (table[2 * t + 1] % rows) ^ row_pos
            picks[r * owners + e] = jnp.full(picks.shape[1:], block % per_device, jnp.int32)
            cols = pl.ds(pl.multiple_of(s * tile, tile), tile)
            dense[r, e, :, cols] = (dense[r, e, :, cols].astype(FULL) + tiles[0, t].astype(FULL)).astype(HALF)
            return carry

        lax.fori_loop(0, table[2 * slots], add, 0)


def project_kernel(own_hbm, peer_hbm, weight_hbm, out, own, peer, weight, sems):
    width = weight.shape[1]
    core = lax.axis_index("col") % 2
    columns = pl.ds(pl.multiple_of(core * width, width), width)
    copies = [
        pltpu.make_async_copy(weight_hbm.at[:, columns], weight, sems.at[0]),
        pltpu.make_async_copy(own_hbm, own, sems.at[1]),
        pltpu.make_async_copy(peer_hbm, peer, sems.at[2]),
    ]
    for copy in copies:
        copy.start()
    for copy in copies:
        copy.wait()
    for r, x in enumerate((own, peer)):
        product = jnp.dot(x[...], weight[...], preferred_element_type=FULL).astype(HALF)
        out[r] = product.reshape(out.shape[1:])


def farthest_last(items):
    return [items[0], *items[:0:-1]]


def select_kernel(*refs, rows):
    needed, values, outs = farthest_last(refs[:rows]), refs[rows], refs[rows + 1 :]
    row_pos = lax.axis_index("row")
    columns = outs[0].shape[-1]
    for s in range(rows):
        for r in range(2):
            block = needed[s][r, row_pos]
            for j in range(len(outs) // rows):
                outs[j * rows + s][r] = values[r, block, :, j * columns : (j + 1) * columns]


def multiply_kernel(*refs):
    picks, dense = refs[:2]
    _, owners, tile, depth = dense.shape
    rows = depth // tile
    pieces, outs = refs[2 : 2 + rows], refs[2 + rows :]
    chips = owners // 2
    columns = outs[0].shape[-1]
    operands = [jnp.concatenate([piece[r] for piece in farthest_last(pieces)], axis=0) for r in range(2)]
    products = [jnp.dot(dense[r].reshape(owners * tile, depth), operands[r], preferred_element_type=FULL) for r in range(2)]
    for e in range(owners):
        own, peer = (product[e * tile : (e + 1) * tile] for product in products)
        for b in range(2):
            total = jnp.where(picks[e, :, :1] == b, own, 0.0) + jnp.where(picks[owners + e, :, :1] == b, peer, 0.0)
            for j in range(len(outs) // chips):
                outs[j * chips + e // 2][e % 2, b] = total[:, j * columns : (j + 1) * columns].astype(HALF)


def added(parts, r, b):
    total = parts[0][r, b].astype(FULL)
    for part in parts[1:]:
        total = total + part[r, b].astype(FULL)
    return total


def hidden_kernel(*refs, rows):
    values = refs[-1]
    needed, parts, outs = farthest_last(refs[:rows]), refs[rows : -1 - rows], refs[-1 - rows : -1]
    row_pos = lax.axis_index("row")
    for r in range(2):
        for b in range(2):
            values[r, b] = jnp.maximum(added(parts, r, b), 0.0).astype(HALF)
    for s, out in enumerate(outs):
        for r in range(2):
            out[r] = values[r, needed[s][r, row_pos]]


def mixed_kernel(*refs):
    parts, own, peer = refs[:-2], refs[-2], refs[-1]
    for b in range(2):
        own[b] = added(parts, 0, b).astype(HALF)
        peer[b] = added(parts, 1, b).astype(HALF)


def final_kernel(*refs):
    weight, out = refs[-2:]
    sides = refs[: len(refs) // 2 - 1], refs[len(refs) // 2 - 1 : -2]
    core = lax.axis_index("col") % 2
    total = None
    for side, chunks in enumerate(sides):
        at = (core ^ side) * (weight.shape[0] // 2)
        for x in chunks:
            width = x.shape[-1]
            rows = x[...].reshape(out.shape[0], width)
            columns = weight[pl.ds(pl.multiple_of(at, width), width), :]
            product = jnp.dot(rows, columns, preferred_element_type=FULL)
            total = product if total is None else total + product
            at = at + width
    out[...] = total.astype(HALF)


def body(features, tile_values, tile_blocks, tile_count, needed, weight_one, weight_two):
    row_count = lax.axis_size("row")
    col_count = lax.axis_size("col")
    chips = col_count // 2
    _, slots, tile, _ = tile_values.shape
    width = features.shape[1] // 2
    limit = min(60, 12 + 3 * (col_count * row_count * tile * tile) // 2**19) * 2**20

    def call(kernel, out_shape, args, in_specs=None, out_specs=None, **options):
        many = isinstance(out_shape, list)
        return pl.pallas_call(
            kernel,
            in_specs=in_specs or [VMEM] * len(args),
            out_specs=out_specs or ([VMEM] * len(out_shape) if many else VMEM),
            out_shape=out_shape,
            compiler_params=pltpu.CompilerParams(vmem_limit_bytes=limit),
            cost_estimate=pl.CostEstimate(flops=FLOPS, bytes_accessed=FLOPS // 100, transcendentals=0),
            **options,
        )(*args)

    def in_hbm(x):
        return pltpu.with_memory_space_constraint(x, pltpu.HBM)

    def by_col(x, masks):
        return lax.ppermute(x, "col", [(i, i ^ masks[i % 2]) for i in range(col_count)])

    def swap(x):
        return by_col(x, (1, 1))

    def by_row(x, s):
        return lax.ppermute(x, "row", [(i, i ^ s) for i in range(row_count)])

    def shape(*dims, dtype=HALF):
        return jax.ShapeDtypeStruct(dims, dtype)

    needs = jnp.concatenate([needed, swap(needed)], axis=0)
    features, tile_values, needs = lax.optimization_barrier((features, tile_values, needs))
    needs = [needs] + [by_row(needs, s) for s in range(row_count - 1, 0, -1)]
    peer_features = swap(features)
    projected = call(
        project_kernel,
        shape(2, 2, tile, width),
        [in_hbm(features), peer_features, in_hbm(weight_one)],
        in_specs=[pl.BlockSpec(memory_space=pltpu.HBM)] * 3,
        scratch_shapes=[
            pltpu.VMEM(features.shape, HALF),
            pltpu.VMEM(features.shape, HALF),
            pltpu.VMEM((features.shape[1], width), HALF),
            pltpu.SemaphoreType.DMA((3,)),
        ],
        name="project",
    )
    tile_blocks, tile_count, projected = lax.optimization_barrier((tile_blocks, tile_count, projected))
    table = jnp.concatenate([tile_blocks.reshape(-1), tile_count])
    dense, picks = call(
        build_kernel,
        [shape(2, col_count, tile, row_count * tile), shape(2 * col_count, 1, tile, dtype=jnp.int32)],
        [table, swap(table), tile_values, swap(tile_values)],
        in_specs=[SMEM] * 2 + [VMEM] * 2,
        name="build",
    )
    columns = width // CHUNKS

    def to_readers(pieces):
        return [pieces[0]] + [by_row(pieces[s], s) for s in range(row_count - 1, 0, -1)]

    def to_owners(pieces):
        chunks = pieces[0].shape[-1] // columns
        parts = call(
            multiply_kernel,
            [shape(2, 2, tile, columns)] * (chips * chunks),
            [picks, dense, *pieces],
            name="multiply",
        )
        parts = [parts[j * chips : (j + 1) * chips] for j in range(chunks)]
        return [[x[0]] + [by_col(x[c], (2 * c, 2 * c)) for c in range(1, chips)] for x in parts]

    selected = call(
        functools.partial(select_kernel, rows=row_count),
        [shape(2, tile, columns)] * (row_count * CHUNKS),
        [*needs, projected],
        in_specs=[SMEM] * row_count + [VMEM],
        name="select",
    )
    panels = [to_readers(selected[j * row_count : (j + 1) * row_count]) for j in range(CHUNKS)]
    arrived = [parts for panel in panels for parts in to_owners(panel)]
    panels = []
    for parts in arrived:
        selected = call(
            functools.partial(hidden_kernel, rows=row_count),
            [shape(2, tile, columns)] * row_count,
            [*needs, *parts],
            in_specs=[SMEM] * row_count + [VMEM] * len(parts),
            scratch_shapes=[pltpu.VMEM((2, 2, tile, columns), HALF)],
            name="hidden",
        )
        panels.append(to_readers(selected))
    arrived = [to_owners(panel)[0] for panel in panels]
    mine, theirs = [], []
    for parts in arrived:
        own, other = call(mixed_kernel, [shape(2, tile, columns)] * 2, parts, name="mixed")
        mine.append(own)
        theirs.append(swap(other))
    return call(final_kernel, shape(*features.shape), [*mine, *theirs, weight_two], name="final")


def solution(mesh):
    placed = (
        P(("row", "col"), None),
        P(("row", "col"), None, None, None),
        P(("row", "col"), None, None),
        P(("row", "col")),
        P(("row", "col"), None),
        P(),
        P(),
    )
    return jax.shard_map(
        body, mesh=mesh, in_specs=placed, out_specs=P(("row", "col"), None), check_vma=False
    )
```

```python
import functools

import jax
import jax.numpy as jnp
from jax import lax
from jax.experimental import pallas as pl
from jax.experimental.pallas import tpu as pltpu
from jax.sharding import PartitionSpec as P

CHUNKS = 2
FLOPS = 1_000_000_000
SMEM = pl.BlockSpec(memory_space=pltpu.SMEM)
VMEM = pl.BlockSpec(memory_space=pltpu.VMEM)
HALF = jnp.bfloat16
FULL = jnp.float32


def build_kernel(own_table, peer_table, own_tiles, peer_tiles, dense, picks):
    _, owners, tile, _ = dense.shape
    slots = own_tiles.shape[1]
    per_device = 2
    rows = dense.shape[3] // tile
    row_pos = lax.axis_index("row")
    col_pos = lax.axis_index("col")
    dense[...] = jnp.zeros_like(dense)
    picks[...] = jnp.zeros_like(picks)
    for r, table, tiles in ((0, own_table, own_tiles), (1, peer_table, peer_tiles)):

        def add(t, carry, r=r, table=table, tiles=tiles):
            block = table[0, 2 * t]
            e = ((block // per_device) % owners) ^ col_pos
            s = (table[0, 2 * t + 1] % rows) ^ row_pos
            picks[r * owners + e] = jnp.full(picks.shape[1:], block % per_device, jnp.int32)
            cols = pl.ds(pl.multiple_of(s * tile, tile), tile)
            dense[r, e, :, cols] = (dense[r, e, :, cols].astype(FULL) + tiles[0, t].astype(FULL)).astype(HALF)
            return carry

        lax.fori_loop(0, table[0, 2 * slots], add, 0)


def project_kernel(own_hbm, peer_hbm, weight_hbm, out, own, peer, weight, sems):
    width = weight.shape[1]
    core = lax.axis_index("col") % 2
    columns = pl.ds(pl.multiple_of(core * width, width), width)
    copies = [
        pltpu.make_async_copy(weight_hbm.at[:, columns], weight, sems.at[0]),
        pltpu.make_async_copy(own_hbm, own, sems.at[1]),
        pltpu.make_async_copy(peer_hbm, peer, sems.at[2]),
    ]
    for copy in copies:
        copy.start()
    for copy in copies:
        copy.wait()
    for r, x in enumerate((own, peer)):
        product = jnp.dot(x[...], weight[...], preferred_element_type=FULL).astype(HALF)
        out[r] = product.reshape(out.shape[1:])


def distances(rows):
    return [0] + sorted(range(1, rows), key=lambda s: s ^ rows // 2)


def by_distance(items):
    order = distances(len(items))
    return [items[order.index(s)] for s in range(len(items))]


def reads_first(needed):
    lane = lax.broadcasted_iota(jnp.int32, needed.shape, 1)
    here = jnp.where(lane == lax.axis_index("row"), needed[...], 0).astype(FULL)
    return jnp.sum(here, axis=1, keepdims=True) < 0.5


def select_kernel(*refs, rows):
    needed, values, outs = by_distance(refs[:rows]), refs[rows], refs[rows + 1 :]
    columns = outs[0].shape[-1]
    for s in range(rows):
        first = reads_first(needed[s])
        for r in range(2):
            block = jnp.where(first[r : r + 1], values[r, 0].astype(FULL), values[r, 1].astype(FULL)).astype(HALF)
            for j in range(len(outs) // rows):
                outs[j * rows + s][r] = block[:, j * columns : (j + 1) * columns]


def multiply_kernel(*refs):
    picks, dense = refs[:2]
    _, owners, tile, depth = dense.shape
    rows = depth // tile
    pieces, outs = refs[2 : 2 + rows], refs[2 + rows :]
    chips = owners // 2
    columns = outs[0].shape[-1]
    operands = [jnp.concatenate([piece[r] for piece in by_distance(pieces)], axis=0) for r in range(2)]
    products = [jnp.dot(dense[r].reshape(owners * tile, depth), operands[r], preferred_element_type=FULL) for r in range(2)]
    for e in range(owners):
        own, peer = (product[e * tile : (e + 1) * tile] for product in products)
        for b in range(2):
            total = jnp.where(picks[e, :, :1] == b, own, 0.0) + jnp.where(picks[owners + e, :, :1] == b, peer, 0.0)
            for j in range(len(outs) // chips):
                outs[j * chips + e // 2][e % 2, b] = total[:, j * columns : (j + 1) * columns].astype(HALF)


def added(parts, r, b):
    total = parts[0][r, b].astype(FULL)
    for part in parts[1:]:
        total = total + part[r, b].astype(FULL)
    return total


def hidden_kernel(*refs, rows):
    needed, parts, outs = by_distance(refs[:rows]), refs[rows:-rows], refs[-rows:]
    firsts = [reads_first(x) for x in needed]
    for r in range(2):
        blocks = [jnp.maximum(added(parts, r, b), 0.0) for b in range(2)]
        for first, out in zip(firsts, outs):
            out[r] = jnp.where(first[r : r + 1], *blocks).astype(HALF)


def mixed_kernel(*refs):
    parts, own, peer = refs[:-2], refs[-2], refs[-1]
    for b in range(2):
        own[b] = added(parts, 0, b).astype(HALF)
        peer[b] = added(parts, 1, b).astype(HALF)


def weighted(chunks, weight, side, start):
    core = lax.axis_index("col") % 2
    at = (core ^ side) * (weight.shape[0] // 2) + start
    total = None
    for x in chunks:
        _, tile, width = x.shape
        rows = weight[pl.ds(pl.multiple_of(at, width), width), :]
        product = jnp.dot(x[...].reshape(2 * tile, width), rows, preferred_element_type=FULL)
        total = product if total is None else total + product
        at = at + width
    return total


def partial_kernel(*refs):
    weight, out = refs[-2:]
    chunks = len(refs) // 2 - 1
    total = weighted(refs[: chunks + 1], weight, 0, 0)
    if chunks:
        total = total + weighted(refs[chunks + 1 : -2], weight, 1, 0)
    out[...] = total


def final_kernel(partial, last, weight, out):
    start = weight.shape[0] // 2 - last.shape[-1]
    out[...] = (partial[...] + weighted([last], weight, 1, start)).astype(HALF)


def body(features, tile_values, tile_blocks, tile_count, needed, weight_one, weight_two):
    row_count = lax.axis_size("row")
    col_count = lax.axis_size("col")
    chips = col_count // 2
    _, slots, tile, _ = tile_values.shape
    width = features.shape[1] // 2
    limit = min(60, 12 + 3 * (col_count * row_count * tile * tile) // 2**19) * 2**20

    def call(kernel, out_shape, args, in_specs=None, out_specs=None, **options):
        many = isinstance(out_shape, list)
        return pl.pallas_call(
            kernel,
            in_specs=in_specs or [VMEM] * len(args),
            out_specs=out_specs or ([VMEM] * len(out_shape) if many else VMEM),
            out_shape=out_shape,
            compiler_params=pltpu.CompilerParams(vmem_limit_bytes=limit),
            cost_estimate=pl.CostEstimate(flops=FLOPS, bytes_accessed=FLOPS // 100, transcendentals=0),
            **options,
        )(*args)

    def in_hbm(x):
        return pltpu.with_memory_space_constraint(x, pltpu.HBM)

    def by_col(x, masks):
        return lax.ppermute(x, "col", [(i, i ^ masks[i % 2]) for i in range(col_count)])

    def swap(x):
        return by_col(x, (1, 1))

    def by_row(x, s):
        return lax.ppermute(x, "row", [(i, i ^ s) for i in range(row_count)])

    def shape(*dims, dtype=HALF):
        return jax.ShapeDtypeStruct(dims, dtype)

    needs = jnp.concatenate([needed, swap(needed)], axis=0)
    features, tile_values, needs = lax.optimization_barrier((features, tile_values, needs))
    needs = [needs] + [by_row(needs, s) for s in distances(row_count)[1:]]
    peer_features = swap(features)
    projected = call(
        project_kernel,
        shape(2, 2, tile, width),
        [in_hbm(features), peer_features, in_hbm(weight_one)],
        in_specs=[pl.BlockSpec(memory_space=pltpu.HBM)] * 3,
        scratch_shapes=[
            pltpu.VMEM(features.shape, HALF),
            pltpu.VMEM(features.shape, HALF),
            pltpu.VMEM((features.shape[1], width), HALF),
            pltpu.SemaphoreType.DMA((3,)),
        ],
        name="project",
    )
    tile_blocks, tile_count, projected = lax.optimization_barrier((tile_blocks, tile_count, projected))
    table = jnp.concatenate([tile_blocks.reshape(1, -1), tile_count.reshape(1, 1)], axis=1)
    dense, picks = call(
        build_kernel,
        [shape(2, col_count, tile, row_count * tile), shape(2 * col_count, 1, tile, dtype=jnp.int32)],
        [table, swap(table), tile_values, swap(tile_values)],
        in_specs=[SMEM] * 2 + [VMEM] * 2,
        name="build",
    )
    columns = width // CHUNKS

    def to_readers(pieces):
        return [pieces[0]] + [by_row(pieces[s], s) for s in distances(row_count)[1:]]

    def to_owners(pieces):
        chunks = pieces[0].shape[-1] // columns
        parts = call(
            multiply_kernel,
            [shape(2, 2, tile, columns)] * (chips * chunks),
            [picks, dense, *pieces],
            name="multiply",
        )
        parts = [parts[j * chips : (j + 1) * chips] for j in range(chunks)]
        return [[x[0]] + [by_col(x[c], (2 * c, 2 * c)) for c in range(1, chips)] for x in parts]

    selected = call(
        functools.partial(select_kernel, rows=row_count),
        [shape(2, tile, columns)] * (row_count * CHUNKS),
        [*needs, projected],
        name="select",
    )
    panels = [to_readers(selected[j * row_count : (j + 1) * row_count]) for j in range(CHUNKS)]
    arrived = [parts for panel in panels for parts in to_owners(panel)]
    panels = []
    for parts in arrived:
        selected = call(
            functools.partial(hidden_kernel, rows=row_count),
            [shape(2, tile, columns)] * row_count,
            [*needs, *parts],
            name="hidden",
        )
        panels.append(to_readers(selected))
    arrived = [to_owners(panel)[0] for panel in panels]
    mine, theirs = [], []
    for parts in arrived:
        own, other = call(mixed_kernel, [shape(2, tile, columns)] * 2, parts, name="mixed")
        mine.append(own)
        theirs.append(swap(other))
    partial = call(
        partial_kernel, shape(*features.shape, dtype=FULL), [*mine, *theirs[:-1], weight_two], name="partial"
    )
    return call(final_kernel, shape(*features.shape), [partial, theirs[-1], weight_two], name="final")


def solution(mesh):
    placed = (
        P(("row", "col"), None),
        P(("row", "col"), None, None, None),
        P(("row", "col"), None, None),
        P(("row", "col")),
        P(("row", "col"), None),
        P(),
        P(),
    )
    return jax.shard_map(
        body, mesh=mesh, in_specs=placed, out_specs=P(("row", "col"), None), check_vma=False
    )
```

```python
import functools

import jax
import jax.numpy as jnp
from jax import lax
from jax.experimental import pallas as pl
from jax.experimental.pallas import tpu as pltpu
from jax.sharding import PartitionSpec as P

CHUNKS = 2
FLOPS = 1_000_000_000
SMEM = pl.BlockSpec(memory_space=pltpu.SMEM)
VMEM = pl.BlockSpec(memory_space=pltpu.VMEM)
HALF = jnp.bfloat16
FULL = jnp.float32


def build_kernel(own_table, peer_table, own_tiles, peer_tiles, dense, picks):
    _, owners, tile, _ = dense.shape
    slots = own_tiles.shape[1]
    per_device = 2
    rows = dense.shape[3] // tile
    row_pos = lax.axis_index("row")
    col_pos = lax.axis_index("col")
    dense[...] = jnp.zeros_like(dense)
    picks[...] = jnp.zeros_like(picks)
    for r, table, tiles in ((0, own_table, own_tiles), (1, peer_table, peer_tiles)):

        def add(t, carry, r=r, table=table, tiles=tiles):
            block = table[0, 2 * t]
            e = ((block // per_device) % owners) ^ col_pos
            s = (table[0, 2 * t + 1] % rows) ^ row_pos
            picks[r * owners + e] = jnp.full(picks.shape[1:], block % per_device, jnp.int32)
            cols = pl.ds(pl.multiple_of(s * tile, tile), tile)
            dense[r, e, :, cols] = (dense[r, e, :, cols].astype(FULL) + tiles[0, t].astype(FULL)).astype(HALF)
            return carry

        lax.fori_loop(0, table[0, 2 * slots], add, 0)


def project_kernel(own_hbm, peer_hbm, weight_hbm, out, own, peer, weight, sems):
    width = weight.shape[1]
    core = lax.axis_index("col") % 2
    columns = pl.ds(pl.multiple_of(core * width, width), width)
    copies = [
        pltpu.make_async_copy(weight_hbm.at[:, columns], weight, sems.at[0]),
        pltpu.make_async_copy(own_hbm, own, sems.at[1]),
        pltpu.make_async_copy(peer_hbm, peer, sems.at[2]),
    ]
    for copy in copies:
        copy.start()
    for copy in copies:
        copy.wait()
    for r, x in enumerate((own, peer)):
        product = jnp.dot(x[...], weight[...], preferred_element_type=FULL).astype(HALF)
        out[r] = product.reshape(out.shape[1:])


def distances(rows, layer=0):
    return [0] + sorted(range(1, rows), key=lambda s: (s != rows // 2, s) if layer else s ^ rows // 2)


def by_distance(items, layer=0):
    order = distances(len(items), layer)
    return [items[order.index(s)] for s in range(len(items))]


def reads_first(needed):
    lane = lax.broadcasted_iota(jnp.int32, needed.shape, 1)
    here = jnp.where(lane == lax.axis_index("row"), needed[...], 0).astype(FULL)
    return jnp.sum(here, axis=1, keepdims=True) < 0.5


def select_kernel(*refs, rows):
    needed, values, outs = by_distance(refs[:rows]), refs[rows], refs[rows + 1 :]
    columns = outs[0].shape[-1]
    for s in range(rows):
        first = reads_first(needed[s])
        for r in range(2):
            block = jnp.where(first[r : r + 1], values[r, 0].astype(FULL), values[r, 1].astype(FULL)).astype(HALF)
            for j in range(len(outs) // rows):
                outs[j * rows + s][r] = block[:, j * columns : (j + 1) * columns]


def multiply_kernel(*refs, layer):
    picks, dense = refs[:2]
    _, owners, tile, depth = dense.shape
    rows = depth // tile
    pieces, outs = refs[2 : 2 + rows], refs[2 + rows :]
    chips = owners // 2
    columns = outs[0].shape[-1]
    operands = [jnp.concatenate([piece[r] for piece in by_distance(pieces, layer)], axis=0) for r in range(2)]
    products = [jnp.dot(dense[r].reshape(owners * tile, depth), operands[r], preferred_element_type=FULL) for r in range(2)]
    for e in range(owners):
        own, peer = (product[e * tile : (e + 1) * tile] for product in products)
        for b in range(2):
            total = jnp.where(picks[e, :, :1] == b, own, 0.0) + jnp.where(picks[owners + e, :, :1] == b, peer, 0.0)
            for j in range(len(outs) // chips):
                outs[j * chips + e // 2][e % 2, b] = total[:, j * columns : (j + 1) * columns].astype(HALF)


def added(parts, r, b):
    total = parts[0][r, b].astype(FULL)
    for part in parts[1:]:
        total = total + part[r, b].astype(FULL)
    return total


def hidden_kernel(*refs, rows):
    needed, parts, outs = by_distance(refs[:rows]), refs[rows:-rows], refs[-rows:]
    firsts = [reads_first(x) for x in needed]
    for r in range(2):
        blocks = [jnp.maximum(added(parts, r, b), 0.0) for b in range(2)]
        for first, out in zip(firsts, outs):
            out[r] = jnp.where(first[r : r + 1], *blocks).astype(HALF)


def mixed_kernel(*refs):
    parts, own, peer = refs[:-2], refs[-2], refs[-1]
    for b in range(2):
        own[b] = added(parts, 0, b).astype(HALF)
        peer[b] = added(parts, 1, b).astype(HALF)


def weighted(chunks, weight, side, start):
    core = lax.axis_index("col") % 2
    at = (core ^ side) * (weight.shape[0] // 2) + start
    total = None
    for x in chunks:
        _, tile, width = x.shape
        rows = weight[pl.ds(pl.multiple_of(at, width), width), :]
        product = jnp.dot(x[...].reshape(2 * tile, width), rows, preferred_element_type=FULL)
        total = product if total is None else total + product
        at = at + width
    return total


def partial_kernel(*refs):
    weight, out = refs[-2:]
    chunks = len(refs) // 2 - 1
    total = weighted(refs[: chunks + 1], weight, 0, 0)
    if chunks:
        total = total + weighted(refs[chunks + 1 : -2], weight, 1, 0)
    out[...] = total


def final_kernel(partial, last, weight, out):
    start = weight.shape[0] // 2 - last.shape[-1]
    out[...] = (partial[...] + weighted([last], weight, 1, start)).astype(HALF)


def body(features, tile_values, tile_blocks, tile_count, needed, weight_one, weight_two):
    row_count = lax.axis_size("row")
    col_count = lax.axis_size("col")
    chips = col_count // 2
    _, slots, tile, _ = tile_values.shape
    width = features.shape[1] // 2
    limit = min(60, 12 + 3 * (col_count * row_count * tile * tile) // 2**19) * 2**20

    def call(kernel, out_shape, args, in_specs=None, out_specs=None, **options):
        many = isinstance(out_shape, list)
        return pl.pallas_call(
            kernel,
            in_specs=in_specs or [VMEM] * len(args),
            out_specs=out_specs or ([VMEM] * len(out_shape) if many else VMEM),
            out_shape=out_shape,
            compiler_params=pltpu.CompilerParams(vmem_limit_bytes=limit),
            cost_estimate=pl.CostEstimate(flops=FLOPS, bytes_accessed=FLOPS // 100, transcendentals=0),
            **options,
        )(*args)

    def in_hbm(x):
        return pltpu.with_memory_space_constraint(x, pltpu.HBM)

    def by_col(x, masks):
        return lax.ppermute(x, "col", [(i, i ^ masks[i % 2]) for i in range(col_count)])

    def swap(x):
        return by_col(x, (1, 1))

    def by_row(x, s):
        return lax.ppermute(x, "row", [(i, i ^ s) for i in range(row_count)])

    def shape(*dims, dtype=HALF):
        return jax.ShapeDtypeStruct(dims, dtype)

    needs = jnp.concatenate([needed, swap(needed)], axis=0)
    features, tile_values, needs = lax.optimization_barrier((features, tile_values, needs))
    needs = [needs] + [by_row(needs, s) for s in distances(row_count)[1:]]
    peer_features = swap(features)
    projected = call(
        project_kernel,
        shape(2, 2, tile, width),
        [in_hbm(features), peer_features, in_hbm(weight_one)],
        in_specs=[pl.BlockSpec(memory_space=pltpu.HBM)] * 3,
        scratch_shapes=[
            pltpu.VMEM(features.shape, HALF),
            pltpu.VMEM(features.shape, HALF),
            pltpu.VMEM((features.shape[1], width), HALF),
            pltpu.SemaphoreType.DMA((3,)),
        ],
        name="project",
    )
    tile_blocks, tile_count, projected = lax.optimization_barrier((tile_blocks, tile_count, projected))
    table = jnp.concatenate([tile_blocks.reshape(1, -1), tile_count.reshape(1, 1)], axis=1)
    dense, picks = call(
        build_kernel,
        [shape(2, col_count, tile, row_count * tile), shape(2 * col_count, 1, tile, dtype=jnp.int32)],
        [table, swap(table), tile_values, swap(tile_values)],
        in_specs=[SMEM] * 2 + [VMEM] * 2,
        name="build",
    )
    columns = width // CHUNKS

    def to_readers(pieces, layer):
        return [pieces[0]] + [by_row(pieces[s], s) for s in distances(row_count, layer)[1:]]

    def to_owners(pieces, layer):
        chunks = pieces[0].shape[-1] // columns
        parts = call(
            functools.partial(multiply_kernel, layer=layer),
            [shape(2, 2, tile, columns)] * (chips * chunks),
            [picks, dense, *pieces],
            name="multiply",
        )
        parts = [parts[j * chips : (j + 1) * chips] for j in range(chunks)]
        return [[x[0]] + [by_col(x[c], (2 * c, 2 * c)) for c in range(1, chips)] for x in parts]

    selected = call(
        functools.partial(select_kernel, rows=row_count),
        [shape(2, tile, columns)] * (row_count * CHUNKS),
        [*needs, projected],
        name="select",
    )
    panels = [to_readers(selected[j * row_count : (j + 1) * row_count], 0) for j in range(CHUNKS)]
    arrived = [parts for panel in panels for parts in to_owners(panel, 0)]
    panels = []
    for parts in arrived:
        selected = call(
            functools.partial(hidden_kernel, rows=row_count),
            [shape(2, tile, columns)] * row_count,
            [*needs, *parts],
            name="hidden",
        )
        panels.append(to_readers(selected, 1))
    arrived = [to_owners(panel, 1)[0] for panel in panels]
    mine, theirs = [], []
    for parts in arrived:
        own, other = call(mixed_kernel, [shape(2, tile, columns)] * 2, parts, name="mixed")
        mine.append(own)
        theirs.append(swap(other))
    partial = call(
        partial_kernel, shape(*features.shape, dtype=FULL), [*mine, *theirs[:-1], weight_two], name="partial"
    )
    return call(final_kernel, shape(*features.shape), [partial, theirs[-1], weight_two], name="final")


def solution(mesh):
    placed = (
        P(("row", "col"), None),
        P(("row", "col"), None, None, None),
        P(("row", "col"), None, None),
        P(("row", "col")),
        P(("row", "col"), None),
        P(),
        P(),
    )
    return jax.shard_map(
        body, mesh=mesh, in_specs=placed, out_specs=P(("row", "col"), None), check_vma=False
    )
```
